32 devices in a mesh: rep: 2 (over x), node: 4 (over z), lane: 4 (over y, core).
Axes of the slice: x: 2, y: 2, z: 4, core: 2. Of those that a mesh axis runs over, the one named last changes fastest.
Arguments:
- moe_rows: bfloat16 [64, 7168], P(('rep', 'node', 'lane')), parts along dimension 0, may hold values from -6 to 6
- expert_ids: int32 [64, 8], P(('rep', 'node', 'lane')), parts along dimension 0, may hold values from 0 to 15, all different within a row; in each aligned block of 2 rows (0 to 1, 2 to 3, ...) at most 2 rows name the same one
- route_scores: float32 [64, 8], P(('rep', 'node', 'lane')), parts along dimension 0, may hold values from 0.05 to 1
- gate_proj: bfloat16 [16, 7168, 2048], P('lane', None, 'node'), may hold values from -0.0625 to 0.0625
- up_proj: bfloat16 [16, 7168, 2048], P('lane', None, 'node'), may hold values from -0.0625 to 0.0625
- down_proj: bfloat16 [16, 2048, 7168], P('lane', 'node'), may hold values from -0.125 to 0.125
Outputs:
- moe_out: bfloat16 [64, 7168], P(('rep', 'node', 'lane')), parts along dimension 0
The draws below stay inside these ranges and needn't reach their ends.
There are 2 independent parts, one for each index of `rep`. The reference program is written for one: setup_inputs(seed, part) draws one part's arguments, and reference() takes and returns one part's arrays. A program takes and returns all parts, laid end to end along the dimension named above; an argument that names none is the same for every part. Nothing has to cross between parts.
Inputs may be any that keep to these rules, and one draw needn't show every extreme that they name: `expert_ids`: each row names 8 different experts; the rows of one device name no expert more than 2 times.
All inputs are finite; a program needn't handle non-finite values.
Results may differ from the reference program's by a relative error of at most 0.012.
Values may be sent and summed in bfloat16 or wider, within the bound.
No kernel may reach another device: no remote copies, remote signals or barrier semaphores. Data moves between devices by JAX's collectives and lax.ppermute only.
A program may use at most 128 MiB of HBM per device.

```python
import math
import jax
import jax.numpy as jnp
import numpy as np
from jax import lax

D = 7168
TOP = 8
FF_WIN = 2048
EXPERTS = 16
T_DEV = 2
CAP = 2
TOKENS = 32
N_NODE = 4


def steps_of(rng, shape, shards, smallest, high):
    gain, own = 1.0, jax.random.fold_in(rng, 6)
    for axis_at, parts in shards:
        heights = jnp.exp(jax.random.uniform(jax.random.fold_in(own, axis_at), (parts,), jnp.float32, smallest / len(shards), high / len(shards)))
        gain = gain * jnp.repeat(heights, shape[axis_at] // parts).reshape([-1 if axis == axis_at else 1 for axis in range(len(shape))])
    return gain


def deal_out(key, own, number, rows, number_of, top, most, lean):
    order = jax.random.permutation(key, number_of)
    crowded, common = shares(number_of, rows * top, most, lean, True), shares(number_of, rows * top, most, lean, False)
    places = jnp.arange(number_of)

    def named(tallies, offset_by):
        used = int((tallies > 0).sum())
        fixed = max(1, used // 4)
        shifted = fixed + (places - fixed + offset_by * (used - fixed)) % max(1, number_of - fixed)
        return jnp.zeros((number_of,), jnp.int32).at[order[jnp.where(places < fixed, places, shifted)]].set(jnp.asarray(tallies, jnp.int32))

    tallies = jnp.where(number % 4 == 0, named(crowded, number // 4), named(common, number - number // 4 - 1))
    mixed = jax.random.permutation(jax.random.fold_in(own, 3), number_of)
    giver, taker = mixed[0:number_of // 2 * 2:2], mixed[1:number_of // 2 * 2:2]
    slack = jnp.minimum(tallies[giver] - 1, most - tallies[taker]) // 2
    slack = jnp.where((giver == order[0]) | (taker == order[0]) | (tallies[taker] == 0), 0, jnp.maximum(slack, 0))
    shifted = jax.random.randint(jax.random.fold_in(own, 4), (number_of // 2,), 0, 1 << 20) % (slack + 1)
    tallies = tallies.at[giver].add(-shifted).at[taker].add(shifted)
    items = jnp.searchsorted(jnp.cumsum(tallies), jnp.arange(rows * top), side="right").astype(jnp.int32)
    listing = items.reshape(top, rows).T
    listing = listing[jax.random.permutation(jax.random.fold_in(own, 1), rows)]
    offset_by = jax.random.randint(jax.random.fold_in(own, 2), (rows, 1), 0, top)
    return jnp.take_along_axis(listing, (jnp.arange(top)[None, :] + offset_by) % top, axis=1)


def shares(number_of, total, bound, lean, full):
    weights = [(1 << 20) // math.isqrt(grade ** lean) + 1 for grade in range(1, number_of + 1)]
    largest = bound if full else min(bound, max(-(-total // number_of), total * weights[0] // sum(weights)))
    least = 1 if total - largest >= number_of - 1 else 0
    holding, surplus = [largest] + [least] * (number_of - 1), total - largest - least * (number_of - 1)
    while surplus > 0:
        free = [i for i in range(1, number_of) if holding[i] < largest] or [i for i in range(1, number_of) if holding[i] < bound]
        whole, left = sum([weights[i] for i in free]), surplus
        for i in free:
            extra = min(bound - holding[i], max(1, left * weights[i] // whole), surplus)
            holding[i] = holding[i] + extra
            surplus = surplus - extra
    return np.array(holding)


def scatter_about(key, shape, spread, reach, shards=(), kind=jnp.bfloat16):
    entries = spread * jax.random.normal(key, shape, jnp.float32)
    if shards:
        entries = entries * steps_of(key, shape, shards, -0.22, 0.18)
    return jnp.clip(entries, -reach, reach).astype(kind)


def setup_inputs(seed: int = 0, part: int = 0) -> dict:
    key_of = jax.random.split(jax.random.key(seed), 7)
    part_keys = jax.random.split(jax.random.fold_in(key_of[6], part), 7)
    moe_rows = scatter_about(part_keys[0], (TOKENS, D), 1.0, 6.0, ((0, 16),))
    expert_ids_keys = jax.random.split(jax.random.fold_in(part_keys[1], 1), TOKENS // T_DEV)
    expert_ids_turns = jax.random.permutation(jax.random.fold_in(part_keys[1], 3), TOKENS // T_DEV)
    expert_ids = jax.vmap(lambda own, number: deal_out(jax.random.fold_in(part_keys[1], 2), own, number, T_DEV, EXPERTS, TOP, CAP, 2))(expert_ids_keys, expert_ids_turns).reshape((TOKENS, TOP))
    route_scores = jnp.clip(0.05 + 0.95 * jax.random.uniform(part_keys[2], (TOKENS, TOP), jnp.float32) ** steps_of(part_keys[2], (TOKENS, TOP), ((0, 16),), -0.2, 0.2), 0.05, 1.0)
    gate_proj = scatter_about(key_of[3], (EXPERTS, D, FF_WIN), D ** -0.5, 0.0625, ((0, 4), (2, 4)))
    up_proj = scatter_about(key_of[4], (EXPERTS, D, FF_WIN), D ** -0.5, 0.0625, ((0, 4), (2, 4)))
    down_proj = scatter_about(key_of[5], (EXPERTS, FF_WIN, D), FF_WIN ** -0.5, 0.125, ((0, 4), (1, 4)))
    return {"moe_rows": moe_rows, "expert_ids": expert_ids, "route_scores": route_scores, "gate_proj": gate_proj, "up_proj": up_proj, "down_proj": down_proj}


route_factor = 2.5


def reference(moe_rows, expert_ids, route_scores, gate_proj, up_proj, down_proj):
    weights = route_factor * route_scores / jnp.sum(route_scores, axis=1, keepdims=True)
    shard_width = FF_WIN // N_NODE

    def one_expert(running, expert_index):
        gate_val = jnp.dot(moe_rows, gate_proj[expert_index], preferred_element_type=jnp.float32)
        up_val = jnp.dot(moe_rows, up_proj[expert_index], preferred_element_type=jnp.float32)
        hidden = (jax.nn.silu(gate_val) * up_val).astype(jnp.bfloat16)
        down_rows = down_proj[expert_index]
        summed = jnp.zeros((TOKENS, D), jnp.float32)
        for shard_index in range(N_NODE):
            lower = shard_index * shard_width
            term = jnp.dot(hidden[:, lower:lower + shard_width], down_rows[lower:lower + shard_width], preferred_element_type=jnp.float32)
            rounded = lax.optimization_barrier(term.astype(jnp.bfloat16))
            summed = summed + rounded.astype(jnp.float32)
        column = jnp.sum(jnp.where(expert_ids == expert_index, weights, 0.0), axis=1)
        return running + column[:, None] * summed, 0

    start_sum = jnp.zeros((TOKENS, D), jnp.float32)
    total_out, unused = lax.scan(one_expert, start_sum, jnp.arange(EXPERTS, dtype=jnp.int32))
    return total_out.astype(jnp.bfloat16)
```

```python
import functools

import jax
import jax.numpy as jnp
from jax import lax
from jax.experimental import pallas as pl
from jax.experimental.pallas import tpu as pltpu
from jax.sharding import PartitionSpec as P

route_factor = 2.5
LANES = 128
ROWS_MXU = 128


def swap(x, axis, bit):
    size = lax.axis_size(axis)
    return lax.ppermute(x, axis, [(i, i ^ bit) for i in range(size)])


def bits_of(size):
    bits, bit = [], size // 2
    while bit:
        bits.append(bit)
        bit //= 2
    return bits


def pack_kernel(experts, rows_ref, ids_ref, scores_ref, out_ref):
    width = rows_ref.shape[1]
    scores = scores_ref[...]
    ids = ids_ref[...]
    weights = route_factor * scores / jnp.sum(scores, axis=1, keepdims=True)
    high = weights.astype(jnp.bfloat16).astype(jnp.float32)
    low = weights - high
    lane = lax.broadcasted_iota(jnp.int32, (ids.shape[0], out_ref.shape[1] - width), 1)
    tail = jnp.zeros(lane.shape, jnp.float32)
    for k in range(ids.shape[1]):
        name = ids[:, k : k + 1]
        tail = tail + jnp.where(lane == name, high[:, k : k + 1], 0.0)
        tail = tail + jnp.where(lane == name + experts, low[:, k : k + 1], 0.0)
    out_ref[:, :width] = rows_ref[...]
    out_ref[:, width:] = tail.astype(jnp.bfloat16)


def pack(rows, ids, scores, experts):
    tail = -(-2 * experts // LANES) * LANES
    return pl.pallas_call(
        functools.partial(pack_kernel, experts),
        out_shape=jax.ShapeDtypeStruct((rows.shape[0], rows.shape[1] + tail), rows.dtype),
        in_specs=[pl.BlockSpec(memory_space=pltpu.VMEM)] * 3,
        out_specs=pl.BlockSpec(memory_space=pltpu.VMEM),
        compiler_params=pltpu.CompilerParams(vmem_limit_bytes=2 << 20),
        name="pack",
    )(rows, ids, scores)


def ffn_kernel(plan, first_ref, *refs):
    experts_here, width, hidden, held, kc, n1, n2, nc, experts = plan
    held_refs, refs = refs[:held], refs[held:]
    (xa_ref, xb_ref, gate_hbm, up_hbm, down_hbm, keep_ref, send_ref, x_buf, tail_buf, h_buf, ring1, ring2, sem1, sem2) = refs
    half = xa_ref.shape[0]
    rows = 2 * half
    ksteps = width // kc
    mats = [(e, m) for e in range(experts_here) for m in range(2)]
    stream = [(e, m, k) for (e, m) in mats[held:] for k in range(ksteps)]
    blocks = width // nc

    def copy1(i):
        e, m, k = stream[i]
        source = (gate_hbm, up_hbm)[m]
        return pltpu.make_async_copy(
            source.at[e, pl.ds(k * kc, kc), :], ring1.at[i % n1], sem1.at[i % n1]
        )

    def copy2(c):
        return pltpu.make_async_copy(
            down_hbm.at[:, :, pl.ds(c * nc, nc)], ring2.at[c % n2], sem2.at[c % n2]
        )

    for i in range(min(n1, len(stream))):
        copy1(i).start()
    for c in range(min(n2, blocks)):
        copy2(c).start()

    x_buf[...] = jnp.zeros_like(x_buf)
    x_buf[:half, :] = xa_ref[:, :width]
    x_buf[half:rows, :] = xb_ref[:, :width]
    tail_buf[:half, :] = xa_ref[:, width:].astype(jnp.float32)
    tail_buf[half:, :] = xb_ref[:, width:].astype(jnp.float32)
    h_buf[...] = jnp.zeros_like(h_buf)
    lane = lax.broadcasted_iota(jnp.int32, tail_buf.shape, 1)

    at = 0
    value = [None, None]
    for index, (e, m) in enumerate(mats):
        if index < held:
            total = jnp.dot(x_buf[...], held_refs[index][0], preferred_element_type=jnp.float32)[:rows]
        else:
            total = jnp.zeros((rows, hidden), jnp.float32)
            for k in range(ksteps):
                copy1(at).wait()
                total = total + jnp.dot(
                    x_buf[:, k * kc : (k + 1) * kc],
                    ring1[at % n1],
                    preferred_element_type=jnp.float32,
                )[:rows]
                if at + n1 < len(stream):
                    copy1(at + n1).start()
                at += 1
        value[m] = total
        if m == 1:
            name = first_ref[0] + e
            mine = jnp.where((lane == name) | (lane == name + experts), tail_buf[...], 0.0)
            weight = jnp.sum(mine, axis=1, keepdims=True)
            gate_val, up_val = value
            h = gate_val / (1.0 + jnp.exp(-gate_val)) * up_val * weight
            h_buf[:rows, e * hidden : (e + 1) * hidden] = h.astype(jnp.bfloat16)

    for c in range(blocks):
        copy2(c).wait()
        total = jnp.dot(
            h_buf[...],
            ring2[c % n2].reshape(experts_here * hidden, nc),
            preferred_element_type=jnp.float32,
        )[:rows].astype(jnp.bfloat16)
        keep_ref[:, c * nc : (c + 1) * nc] = total[:half]
        send_ref[:, c * nc : (c + 1) * nc] = total[half:]
        if c + n2 < blocks:
            copy2(c + n2).start()


def ffn(xa, xb, gate_proj, up_proj, down_proj, first, experts, held=0, kc=1792, n1=6, n2=4, nc=512):
    experts_here, width, hidden = gate_proj.shape
    held = min(held, 2 * experts_here)
    half = xa.shape[0]
    ready = [
        pltpu.with_memory_space_constraint(lax.slice_in_dim((gate_proj, up_proj)[i % 2], i // 2, i // 2 + 1), pltpu.VMEM)
        for i in range(held)
    ]
    any_spec = pl.BlockSpec(memory_space=pl.ANY)
    vmem_spec = pl.BlockSpec(memory_space=pltpu.VMEM)
    rows_mxu = max(ROWS_MXU, -(-2 * half // 16) * 16)
    out = jax.ShapeDtypeStruct((half, width), jnp.bfloat16)
    bytes_all = 3 * gate_proj.size * 2
    return pl.pallas_call(
        functools.partial(ffn_kernel, (experts_here, width, hidden, held, kc, n1, n2, nc, experts)),
        out_shape=(out, out),
        in_specs=[pl.BlockSpec(memory_space=pltpu.SMEM)] + [vmem_spec] * held + [vmem_spec] * 2 + [any_spec] * 3,
        out_specs=(vmem_spec, vmem_spec),
        scratch_shapes=[
            pltpu.VMEM((rows_mxu, width), jnp.bfloat16),
            pltpu.VMEM((2 * half, xa.shape[1] - width), jnp.float32),
            pltpu.VMEM((rows_mxu, experts_here * hidden), jnp.bfloat16),
            pltpu.VMEM((n1, kc, hidden), jnp.bfloat16),
            pltpu.VMEM((n2, experts_here, hidden, nc), jnp.bfloat16),
            pltpu.SemaphoreType.DMA((n1,)),
            pltpu.SemaphoreType.DMA((n2,)),
        ],
        compiler_params=pltpu.CompilerParams(vmem_limit_bytes=27 << 20),
        cost_estimate=pl.CostEstimate(flops=2 * half * bytes_all, bytes_accessed=bytes_all, transcendentals=0),
        name="ffn",
    )(first, *ready, xa, xb, gate_proj, up_proj, down_proj)


def on_device(moe_rows, expert_ids, route_scores, gate_proj, up_proj, down_proj):
    lanes = lax.axis_size("lane")
    experts_here = gate_proj.shape[0]
    experts = experts_here * lanes
    steps = [("node", b) for b in bits_of(lax.axis_size("node"))] + [("lane", b) for b in bits_of(lanes)]
    mine = pack(moe_rows, expert_ids, route_scores, experts)
    for axis, bit in steps[:-1]:
        mine = jnp.concatenate([mine, swap(mine, axis, bit)])
    other = swap(mine, *steps[-1])
    first = (lax.axis_index("lane") * experts_here).astype(jnp.int32).reshape((1,))
    keep, send = ffn(mine, other, gate_proj, up_proj, down_proj, first, experts)
    keep = keep + swap(send, *steps[-1])
    for axis, bit in reversed(steps[:-1]):
        half = keep.shape[0] // 2
        keep = keep[:half] + swap(keep[half:], axis, bit)
    return keep


def solution(mesh):
    in_specs = (
        P(("rep", "node", "lane"), None),
        P(("rep", "node", "lane"), None),
        P(("rep", "node", "lane"), None),
        P("lane", None, "node"),
        P("lane", None, "node"),
        P("lane", "node", None),
    )
    out_specs = P(("rep", "node", "lane"), None)
    return jax.shard_map(
        on_device, mesh=mesh, in_specs=in_specs, out_specs=out_specs, check_vma=False
    )
```
